512 devices in a mesh: segment: 8 (over z_lo), seq: 16 (over z_hi, y, core), head: 4 (over x).
Axes of the slice: x: 4, y: 4, z: 16 (z_hi: 2, z_lo: 8; z = z_hi * 8 + z_lo), core: 2. Of those that a mesh axis runs over, the one named last changes fastest.
Arguments:
- tokens: bfloat16 [8, 4096, 1536], P('segment', ('seq', 'head'))
- lengths: int32 [8], replicated, may hold values from 2048 to 4096, as said below
- modulation: bfloat16 [8, 2, 1536], P('segment'), may hold values from -0.5 to 0.5
- gate_gain: bfloat16 [8, 1536], P('segment'), may hold values from 1 to 3
- w_qkv: bfloat16 [8, 1536, 3, 1536], P('segment', None, None, 'head')
- w_out: bfloat16 [8, 1536, 1536], P('segment', 'head'), may hold values from -0.15625 to 0.15625
Outputs:
- states: bfloat16 [8, 4096, 1536], P('segment', ('seq', 'head'))
The draws below stay inside these ranges and needn't reach their ends.
Inputs may be any that keep to these rules, and one draw needn't show every extreme that they name: Micro-batch m has lengths[m] real tokens at the start of its 4096 slots; some micro-batch fills all 4096.
All inputs are finite; a program needn't handle non-finite values.
Results may differ from the reference program's by a relative error of at most 0.02.
Values may be sent and summed in bfloat16 or wider, within the bound.
A program may use at most 64 MiB of HBM per device.

```python
import math
import jax
import jax.numpy as jnp
from jax import lax

D = 1536
HEAD = 128
HEADS = 12
TICKS = 2
SECTIONS = 8
MICRO = 8
SEQ = 4096


def draw_tokens(key, part):
    full_shape = (MICRO, SEQ, D)
    drawn = jax.random.normal(key, full_shape, jnp.float32)
    return drawn.astype(jnp.bfloat16)


def draw_lengths(key, part):
    lengths_drawn = jax.random.randint(key, (MICRO,), SEQ // 2, SEQ + 1)
    full_index = jax.random.randint(jax.random.fold_in(key, 5), (), 0, MICRO)
    return jnp.where(jnp.arange(MICRO) == full_index, SEQ, lengths_drawn).astype(jnp.int32)


def draw_w_qkv(key, part):
    full_shape = (SECTIONS, D, 3, HEADS * HEAD)
    scales = jnp.array([math.sqrt(2.0 / D), math.sqrt(2.0 / D), math.sqrt(1.0 / D)], jnp.float32)
    drawn = jax.random.normal(key, full_shape, jnp.float32) * scales[None, None, :, None]
    return drawn.astype(jnp.bfloat16)


def levels(rng, shape, pieces, least, top_value):
    loudness = 1.0
    for axis_at, blocks in pieces:
        heights = jax.random.uniform(jax.random.fold_in(jax.random.fold_in(rng, 6), axis_at), (blocks,), jnp.float32, least / len(pieces), top_value / len(pieces))
        loudness = loudness * jnp.repeat(jnp.exp(heights), shape[axis_at] // blocks).reshape((-1,) + (1,) * (len(shape) - 1 - axis_at))
    return loudness


def noise(stream_key, shape, spread, reach, shards=(), kind=jnp.bfloat16):
    entries = spread * jax.random.normal(stream_key, shape, jnp.float32)
    if shards:
        entries = entries * levels(stream_key, shape, shards, -0.22, 0.18)
    return jnp.clip(entries, -reach, reach).astype(kind)


def setup_inputs(seed: int = 0) -> dict:
    splits = jax.random.split(jax.random.key(seed), 7)
    return {
        "tokens": draw_tokens(jax.random.fold_in(splits[6], 71), 0),
        "lengths": draw_lengths(jax.random.fold_in(splits[6], 71), 0),
        "modulation": jnp.clip(jax.random.uniform(splits[2], (SECTIONS, 2, D), jnp.float32, -0.5, 0.5) * levels(splits[2], (SECTIONS, 2, D), ((0, 8),), -0.4, 0.0), -0.5, 0.5).astype(jnp.bfloat16),
        "gate_gain": jnp.clip(1.0 + 2.0 * jax.random.uniform(splits[3], (SECTIONS, D), jnp.float32) ** levels(splits[3], (SECTIONS, D), ((0, 8),), -0.2, 0.2), 1.0, 3.0).astype(jnp.bfloat16),
        "w_qkv": draw_w_qkv(jax.random.fold_in(splits[6], 71), 0),
        "w_out": noise(splits[5], (SECTIONS, HEADS * HEAD, D), (HEADS * HEAD) ** -0.5, 0.15625, ((0, 8), (1, 4))),
    }


def layer_norm(values):
    row_mean = lax.optimization_barrier(jnp.mean(values, axis=-1, keepdims=True))
    centered = values - row_mean
    row_var = lax.optimization_barrier(jnp.mean(centered * centered, axis=-1, keepdims=True))
    return centered / jnp.sqrt(row_var + 1e-06)

def section(state, length, shift_scale, gate_row, qkv_matrix, out_matrix):
    values = state.astype(jnp.float32)
    shift_scale = shift_scale.astype(jnp.float32)
    normed = (layer_norm(values) * (1.0 + shift_scale[1]) + shift_scale[0]).astype(jnp.bfloat16)
    head_width = qkv_matrix.shape[2]
    projected = jnp.dot(normed, qkv_matrix.reshape(qkv_matrix.shape[0], 3 * head_width), preferred_element_type=jnp.float32).astype(jnp.bfloat16)
    projected = projected.reshape(SEQ, 3, HEADS, HEAD)
    queries = jnp.transpose(projected[:, 0], (1, 0, 2))
    keys = jnp.transpose(projected[:, 1], (1, 0, 2))
    value_rows = jnp.transpose(projected[:, 2], (1, 0, 2))
    key_valid = jnp.arange(SEQ) < length

    def one_head(inputs):
        query_head, key_head, value_head = inputs
        scores = jnp.dot(query_head, key_head.T, preferred_element_type=jnp.float32) * HEAD ** (-0.5)
        scores = jnp.where(key_valid[None, :], scores, -1e+30)
        row_max = lax.optimization_barrier(jnp.max(scores, axis=1, keepdims=True))
        exponent = jnp.where(key_valid[None, :], jnp.exp(scores - row_max), 0.0)
        row_sum = lax.optimization_barrier(jnp.sum(exponent, axis=1, keepdims=True))
        weighted = jnp.dot(exponent.astype(jnp.bfloat16), value_head, preferred_element_type=jnp.float32)
        return (weighted / row_sum).astype(jnp.bfloat16)
    attended = lax.map(one_head, (queries, keys, value_rows))
    attended = jnp.transpose(attended, (1, 0, 2)).reshape(SEQ, HEADS * HEAD)
    branch = jnp.dot(attended, out_matrix, preferred_element_type=jnp.float32)
    return (values + gate_row.astype(jnp.float32) * branch).astype(jnp.bfloat16)

def reference(tokens, lengths, modulation, gate_gain, w_qkv, w_out):
    states = tokens
    for tick_index in range(TICKS):
        results = []
        for position in range(MICRO):
            micro_index = (position - tick_index) % MICRO
            results.append(section(states[position], lengths[micro_index], modulation[position], gate_gain[position], w_qkv[position], w_out[position]))
        states = jnp.roll(jnp.stack(results), 1, axis=0)
    return states
```

```python
import functools
import math

import jax
import jax.numpy as jnp
from jax import lax
from jax.experimental import pallas as pl
from jax.experimental.pallas import tpu as pltpu
from jax.sharding import PartitionSpec as P

HEAD = 128
TICKS = 2
PLANE = 8
KEY_BLOCK = 1024
EXP2_SCALE = HEAD ** (-0.5) * math.log2(math.e)


def layer_norm(values):
    row_mean = jnp.mean(values, axis=-1, keepdims=True)
    centered = values - row_mean
    row_var = jnp.mean(centered * centered, axis=-1, keepdims=True)
    return centered / jnp.sqrt(row_var + 1e-06)


def attend_kernel(info_ref, q_ref, k_ref, v_ref, o_ref, max_ref, sum_ref, acc_ref):
    step = pl.program_id(1)
    length = info_ref[0]
    half = info_ref[1]

    @pl.when(step == 0)
    def _():
        max_ref[...] = jnp.full_like(max_ref, -1e30)
        sum_ref[...] = jnp.zeros_like(sum_ref)
        acc_ref[...] = jnp.zeros_like(acc_ref)

    row = lax.broadcasted_iota(jnp.int32, (1, KEY_BLOCK), 1) + step * KEY_BLOCK
    slot = jnp.bitwise_and(jnp.right_shift(row, 6), 1)
    which = jnp.bitwise_xor(slot, half)
    source = jnp.right_shift(row, 7)
    position = which * 2048 + source * 64 + jnp.bitwise_and(row, 63)
    valid = position < length

    scores = lax.dot_general(
        q_ref[...], k_ref[...], (((1,), (1,)), ((), ())), preferred_element_type=jnp.float32
    )
    scores = jnp.where(valid, scores * EXP2_SCALE, -1e30)
    old_max = max_ref[...]
    new_max = jnp.maximum(old_max, jnp.max(scores, axis=1, keepdims=True))
    rescale = jnp.exp2(old_max - new_max)
    weights = jnp.exp2(scores - new_max[:, :1])
    max_ref[...] = new_max
    sum_ref[...] = sum_ref[...] * rescale + jnp.sum(weights, axis=1, keepdims=True)
    acc_ref[...] = acc_ref[...] * rescale + jnp.dot(
        weights.astype(jnp.bfloat16), v_ref[...], preferred_element_type=jnp.float32
    )

    @pl.when(step == pl.num_programs(1) - 1)
    def _():
        o_ref[...] = (acc_ref[...] / sum_ref[...]).astype(o_ref.dtype)


def attend(info, queries, key_value):
    rows, width = queries.shape
    keys = key_value.shape[0]
    heads = width // HEAD
    return pl.pallas_call(
        attend_kernel,
        grid=(heads, keys // KEY_BLOCK),
        in_specs=[
            pl.BlockSpec(memory_space=pltpu.SMEM),
            pl.BlockSpec((rows, HEAD), lambda h, b: (0, h)),
            pl.BlockSpec((KEY_BLOCK, HEAD), lambda h, b: (b, h)),
            pl.BlockSpec((KEY_BLOCK, HEAD), lambda h, b: (b, heads + h)),
        ],
        out_specs=pl.BlockSpec((rows, HEAD), lambda h, b: (0, h)),
        out_shape=jax.ShapeDtypeStruct((rows, width), jnp.bfloat16),
        scratch_shapes=[pltpu.VMEM((rows, HEAD), jnp.float32)] * 3,
    )(info, queries, key_value, key_value)


def per_device(tokens, lengths, modulation, gate_gain, w_qkv, w_out):
    segment_count = lax.axis_size("segment")
    seq_count = lax.axis_size("seq")
    position = lax.axis_index("segment")
    half = lax.axis_index("seq") // PLANE
    groups = [list(range(PLANE)), list(range(PLANE, 2 * PLANE))]
    shift_scale = modulation[0].astype(jnp.float32)
    gate_row = gate_gain[0].astype(jnp.float32)
    model_width = w_qkv.shape[1]
    local_width = w_qkv.shape[3]
    flat_qkv = w_qkv[0].reshape(model_width, 3 * local_width)
    out_rows = w_out[0]
    own = tokens[0]
    other = lax.ppermute(own, "seq", [(i, (i + PLANE) % seq_count) for i in range(seq_count)])
    for tick_index in range(TICKS):
        micro_index = (position - tick_index) % segment_count
        length = lax.dynamic_index_in_dim(lengths, micro_index, 0, keepdims=False)
        info = jnp.stack([length, half.astype(jnp.int32)])
        values = own.astype(jnp.float32)
        both = jnp.concatenate([own, other], axis=0).astype(jnp.float32)
        normed = (layer_norm(both) * (1.0 + shift_scale[1]) + shift_scale[0]).astype(jnp.bfloat16)
        rows = lax.all_gather(normed, "head", axis=0, tiled=True)
        projected = jnp.dot(rows, flat_qkv, preferred_element_type=jnp.float32).astype(jnp.bfloat16)
        tile = own.shape[0]
        queries = projected[:, :local_width].reshape(-1, 2, tile, local_width)[:, 0]
        queries = queries.reshape(-1, local_width)
        key_value = lax.all_gather(
            projected[:, local_width:], "seq", axis=0, tiled=True, axis_index_groups=groups
        )
        attended = attend(info, queries, key_value)
        branch = lax.psum_scatter(
            jnp.dot(attended, out_rows, preferred_element_type=jnp.float32).astype(jnp.bfloat16),
            "head",
            scatter_dimension=0,
            tiled=True,
        ).astype(jnp.float32)
        updated = (values + gate_row * branch).astype(jnp.bfloat16)
        own = lax.ppermute(
            updated, "segment", [(i, (i + 1) % segment_count) for i in range(segment_count)]
        )
        if tick_index + 1 < TICKS:
            other = lax.ppermute(
                updated,
                ("segment", "seq"),
                [
                    (s * seq_count + q, (s + 1) % segment_count * seq_count + (q + PLANE) % seq_count)
                    for s in range(segment_count)
                    for q in range(seq_count)
                ],
            )
    return own[None]


def solution(mesh):
    return jax.shard_map(
        per_device,
        mesh=mesh,
        in_specs=(
            P("segment", ("seq", "head"), None),
            P(),
            P("segment", None, None),
            P("segment", None),
            P("segment", None, None, "head"),
            P("segment", "head", None),
        ),
        out_specs=P("segment", ("seq", "head"), None),
        check_vma=False,
    )
```

```python
import math

import jax
import jax.numpy as jnp
from jax import lax
from jax.experimental import pallas as pl
from jax.experimental.pallas import tpu as pltpu
from jax.sharding import PartitionSpec as P

HEAD = 128
TICKS = 2
PLANE = 8
MESH = pl.DeviceIdType.MESH
EXP2_SCALE = HEAD ** (-0.5) * math.log2(math.e)


def layer_norm(values):
    row_mean = jnp.mean(values, axis=-1, keepdims=True)
    centered = values - row_mean
    row_var = jnp.mean(centered * centered, axis=-1, keepdims=True)
    return centered / jnp.sqrt(row_var + 1e-06)


def barrier(peers):
    sem = pltpu.get_barrier_semaphore()
    for peer in peers:
        pl.semaphore_signal(sem, inc=1, device_id=peer, device_id_type=MESH)
    pl.semaphore_wait(sem, len(peers))


def remote(src, dst, send_sem, recv_sem, index, peer):
    return pltpu.make_async_remote_copy(
        src_ref=src,
        dst_ref=dst,
        send_sem=send_sem.at[index],
        recv_sem=recv_sem.at[index],
        device_id=peer,
        device_id_type=MESH,
    )


def head_gather_kernel(block_ref, out_ref, send_sem, recv_sem, local_sem):
    me = lax.axis_index("head")
    right = lax.rem(me + 1, 4)
    left = lax.rem(me + 3, 4)
    rows = block_ref.shape[0]
    first, second = pl.ds(0, rows // 2), pl.ds(rows // 2, rows // 2)
    barrier([{"head": left}, {"head": right}])
    keep = pltpu.make_async_copy(block_ref, out_ref.at[me], local_sem)
    right_first = remote(block_ref.at[first], out_ref.at[me, first], send_sem, recv_sem, 0, {"head": right})
    left_second = remote(block_ref.at[second], out_ref.at[me, second], send_sem, recv_sem, 1, {"head": left})
    right_second = remote(block_ref.at[second], out_ref.at[me, second], send_sem, recv_sem, 2, {"head": right})
    left_first = remote(block_ref.at[first], out_ref.at[me, first], send_sem, recv_sem, 3, {"head": left})
    on_right = remote(out_ref.at[left, first], out_ref.at[left, first], send_sem, recv_sem, 4, {"head": right})
    on_left = remote(out_ref.at[right, second], out_ref.at[right, second], send_sem, recv_sem, 5, {"head": left})
    right_first.start()
    left_second.start()
    right_second.start()
    left_first.start()
    keep.start()
    right_first.wait_recv()
    on_right.start()
    left_second.wait_recv()
    on_left.start()
    right_second.wait_recv()
    left_first.wait_recv()
    on_right.wait_recv()
    on_left.wait_recv()
    keep.wait()
    for copy in (right_first, left_second, right_second, left_first, on_right, on_left):
        copy.wait_send()


def head_gather(block):
    rows, width = block.shape
    return pl.pallas_call(
        head_gather_kernel,
        out_shape=jax.ShapeDtypeStruct((4, rows, width), block.dtype),
        in_specs=[pl.BlockSpec(memory_space=pltpu.VMEM)],
        out_specs=pl.BlockSpec(memory_space=pltpu.VMEM),
        scratch_shapes=[
            pltpu.SemaphoreType.DMA((6,)),
            pltpu.SemaphoreType.DMA((6,)),
            pltpu.SemaphoreType.DMA,
        ],
        compiler_params=pltpu.CompilerParams(collective_id=0, has_side_effects=True),
    )(block)


def attend_kernel(length_ref, q_ref, kv_ref, o_ref, buf, max_ref, sum_ref, acc_ref, send_sem, recv_sem):
    seq = lax.axis_index("seq")
    half = lax.div(seq, PLANE)
    y = lax.rem(lax.div(seq, 2), 4)
    core = lax.rem(seq, 2)
    base = half * PLANE
    right = {"seq": base + lax.rem(y + 1, 4) * 2 + core}
    left = {"seq": base + lax.rem(y + 3, 4) * 2 + core}
    partner = {"seq": base + y * 2 + (1 - core)}
    rows = kv_ref.shape[0]
    heads = q_ref.shape[1] // HEAD
    first, second = pl.ds(0, rows // 2), pl.ds(rows // 2, rows // 2)
    length = length_ref[0]

    barrier([left, right, partner])
    right_first = remote(kv_ref.at[first], buf.at[3, 0, first], send_sem, recv_sem, 0, right)
    left_second = remote(kv_ref.at[second], buf.at[1, 0, second], send_sem, recv_sem, 1, left)
    right_second = remote(kv_ref.at[second], buf.at[3, 0, second], send_sem, recv_sem, 2, right)
    left_first = remote(kv_ref.at[first], buf.at[1, 0, first], send_sem, recv_sem, 3, left)
    across_own = remote(kv_ref, buf.at[0, 1], send_sem, recv_sem, 4, partner)
    on_right = remote(buf.at[3, 0, first], buf.at[2, 0, first], send_sem, recv_sem, 5, right)
    on_left = remote(buf.at[1, 0, second], buf.at[2, 0, second], send_sem, recv_sem, 6, left)
    across_left = remote(buf.at[3, 0], buf.at[3, 1], send_sem, recv_sem, 7, partner)
    across_right = remote(buf.at[1, 0], buf.at[1, 1], send_sem, recv_sem, 8, partner)
    across_first = remote(buf.at[2, 0, first], buf.at[2, 1, first], send_sem, recv_sem, 9, partner)
    across_second = remote(buf.at[2, 0, second], buf.at[2, 1, second], send_sem, recv_sem, 10, partner)

    def attend_shard(shard, distance, other_core):
        source = lax.rem(y + distance, 4) * 2 + lax.rem(core + other_core, 2)
        row = lax.broadcasted_iota(jnp.int32, (1, rows), 1)
        slot = jnp.bitwise_and(jnp.right_shift(row, 6), 1)
        which = jnp.bitwise_xor(slot, half)
        position = which * 2048 + source * 256 + jnp.right_shift(row, 7) * 64 + jnp.bitwise_and(row, 63)
        valid = position < length

        def one_head(h, carry):
            k_columns = pl.ds(pl.multiple_of(h * HEAD, HEAD), HEAD)
            v_columns = pl.ds(pl.multiple_of((heads + h) * HEAD, HEAD), HEAD)
            scores = lax.dot_general(
                q_ref[:, k_columns],
                shard[:, k_columns],
                (((1,), (1,)), ((), ())),
                preferred_element_type=jnp.float32,
            )
            scores = jnp.where(valid, scores * EXP2_SCALE, -1e30)
            old_max = max_ref[h]
            new_max = jnp.maximum(old_max, jnp.max(scores, axis=1, keepdims=True))
            rescale = jnp.exp2(old_max - new_max)
            weights = jnp.exp2(scores - new_max[:, :1])
            max_ref[h] = new_max
            sum_ref[h] = sum_ref[h] * rescale + jnp.sum(weights, axis=1, keepdims=True)
            acc_ref[h] = acc_ref[h] * rescale + jnp.dot(
                weights.astype(jnp.bfloat16), shard[:, v_columns], preferred_element_type=jnp.float32
            )
            return carry

        lax.fori_loop(0, heads, one_head, 0)

    right_first.start()
    left_second.start()
    right_second.start()
    left_first.start()
    across_own.start()
    max_ref[...] = jnp.full_like(max_ref, -1e30)
    sum_ref[...] = jnp.zeros_like(sum_ref)
    acc_ref[...] = jnp.zeros_like(acc_ref)
    attend_shard(kv_ref, 0, 0)
    right_first.wait_recv()
    on_right.start()
    left_second.wait_recv()
    on_left.start()
    across_own.wait_recv()
    attend_shard(buf.at[0, 1], 0, 1)
    right_second.wait_recv()
    across_left.start()
    left_first.wait_recv()
    across_right.start()
    attend_shard(buf.at[3, 0], 3, 0)
    attend_shard(buf.at[1, 0], 1, 0)
    on_right.wait_recv()
    across_first.start()
    on_left.wait_recv()
    across_second.start()
    across_left.wait_recv()
    attend_shard(buf.at[3, 1], 3, 1)
    across_right.wait_recv()
    attend_shard(buf.at[1, 1], 1, 1)
    attend_shard(buf.at[2, 0], 2, 0)
    across_first.wait_recv()
    across_second.wait_recv()
    attend_shard(buf.at[2, 1], 2, 1)
    for h in range(heads):
        o_ref[:, h * HEAD : (h + 1) * HEAD] = (acc_ref[h] / sum_ref[h]).astype(o_ref.dtype)
    for copy in (
        right_first,
        left_second,
        right_second,
        left_first,
        across_own,
        on_right,
        on_left,
        across_left,
        across_right,
        across_first,
        across_second,
    ):
        copy.wait_send()


def attend(length, queries, key_value):
    rows, width = queries.shape
    heads = width // HEAD
    stats = pltpu.VMEM((heads, rows, HEAD), jnp.float32)
    return pl.pallas_call(
        attend_kernel,
        in_specs=[
            pl.BlockSpec(memory_space=pltpu.SMEM),
            pl.BlockSpec(memory_space=pltpu.VMEM),
            pl.BlockSpec(memory_space=pltpu.VMEM),
        ],
        out_specs=pl.BlockSpec(memory_space=pltpu.VMEM),
        out_shape=jax.ShapeDtypeStruct((rows, width), jnp.bfloat16),
        scratch_shapes=[
            pltpu.VMEM((4, 2) + key_value.shape, key_value.dtype),
            stats,
            stats,
            stats,
            pltpu.SemaphoreType.DMA((11,)),
            pltpu.SemaphoreType.DMA((11,)),
        ],
        compiler_params=pltpu.CompilerParams(collective_id=1, has_side_effects=True),
    )(length, queries, key_value)


def per_device(tokens, lengths, modulation, gate_gain, w_qkv, w_out):
    segment_count = lax.axis_size("segment")
    seq_count = lax.axis_size("seq")
    position = lax.axis_index("segment")
    shift_scale = modulation[0].astype(jnp.float32)
    gate_row = gate_gain[0].astype(jnp.float32)
    model_width = w_qkv.shape[1]
    local_width = w_qkv.shape[3]
    flat_qkv = w_qkv[0].reshape(model_width, 3 * local_width)
    out_rows = w_out[0]
    own = tokens[0]
    other = lax.ppermute(own, "seq", [(i, (i + PLANE) % seq_count) for i in range(seq_count)])
    for tick_index in range(TICKS):
        micro_index = (position - tick_index) % segment_count
        length = lax.dynamic_index_in_dim(lengths, micro_index, 0, keepdims=False)
        values = own.astype(jnp.float32)
        both = jnp.concatenate([own, other], axis=0).astype(jnp.float32)
        normed = (layer_norm(both) * (1.0 + shift_scale[1]) + shift_scale[0]).astype(jnp.bfloat16)
        rows = head_gather(normed).reshape(-1, model_width)
        projected = jnp.dot(rows, flat_qkv, preferred_element_type=jnp.float32).astype(jnp.bfloat16)
        tile = own.shape[0]
        queries = projected[:, :local_width].reshape(-1, 2, tile, local_width)[:, 0]
        queries = queries.reshape(-1, local_width)
        attended = attend(length[None], queries, projected[:, local_width:])
        branch = lax.psum_scatter(
            jnp.dot(attended, out_rows, preferred_element_type=jnp.float32).astype(jnp.bfloat16),
            "head",
            scatter_dimension=0,
            tiled=True,
        ).astype(jnp.float32)
        updated = (values + gate_row * branch).astype(jnp.bfloat16)
        own = lax.ppermute(
            updated, "segment", [(i, (i + 1) % segment_count) for i in range(segment_count)]
        )
        if tick_index + 1 < TICKS:
            other = lax.ppermute(
                updated,
                ("segment", "seq"),
                [
                    (s * seq_count + q, (s + 1) % segment_count * seq_count + (q + PLANE) % seq_count)
                    for s in range(segment_count)
                    for q in range(seq_count)
                ],
            )
    return own[None]


def solution(mesh):
    return jax.shard_map(
        per_device,
        mesh=mesh,
        in_specs=(
            P("segment", ("seq", "head"), None),
            P(),
            P("segment", None, None),
            P("segment", None),
            P("segment", None, None, "head"),
            P("segment", "head", None),
        ),
        out_specs=P("segment", ("seq", "head"), None),
        check_vma=False,
    )
```

```python
import math

import jax
import jax.numpy as jnp
from jax import lax
from jax.experimental import pallas as pl
from jax.experimental.pallas import tpu as pltpu
from jax.sharding import PartitionSpec as P

HEAD = 128
TICKS = 2
PLANE = 8
MESH = pl.DeviceIdType.MESH
EXP2_SCALE = HEAD ** (-0.5) * math.log2(math.e)


def layer_norm(values):
    row_mean = jnp.mean(values, axis=-1, keepdims=True)
    centered = values - row_mean
    row_var = jnp.mean(centered * centered, axis=-1, keepdims=True)
    return centered / jnp.sqrt(row_var + 1e-06)


def barrier(peers):
    sem = pltpu.get_barrier_semaphore()
    for peer in peers:
        pl.semaphore_signal(sem, inc=1, device_id=peer, device_id_type=MESH)
    pl.semaphore_wait(sem, len(peers))


def remote(src, dst, send_sem, recv_sem, index, peer):
    return pltpu.make_async_remote_copy(
        src_ref=src,
        dst_ref=dst,
        send_sem=send_sem.at[index],
        recv_sem=recv_sem.at[index],
        device_id=peer,
        device_id_type=MESH,
    )


def head_gather_kernel(block_ref, out_ref, send_sem, recv_sem, local_sem):
    me = lax.axis_index("head")
    right = lax.rem(me + 1, 4)
    left = lax.rem(me + 3, 4)
    rows = block_ref.shape[0]
    first, second = pl.ds(0, rows // 2), pl.ds(rows // 2, rows // 2)
    barrier([{"head": left}, {"head": right}])
    keep = pltpu.make_async_copy(block_ref, out_ref.at[me], local_sem)
    right_first = remote(block_ref.at[first], out_ref.at[me, first], send_sem, recv_sem, 0, {"head": right})
    left_second = remote(block_ref.at[second], out_ref.at[me, second], send_sem, recv_sem, 1, {"head": left})
    right_second = remote(block_ref.at[second], out_ref.at[me, second], send_sem, recv_sem, 2, {"head": right})
    left_first = remote(block_ref.at[first], out_ref.at[me, first], send_sem, recv_sem, 3, {"head": left})
    on_right = remote(out_ref.at[left, first], out_ref.at[left, first], send_sem, recv_sem, 4, {"head": right})
    on_left = remote(out_ref.at[right, second], out_ref.at[right, second], send_sem, recv_sem, 5, {"head": left})
    right_first.start()
    left_second.start()
    right_second.start()
    left_first.start()
    keep.start()
    right_first.wait_recv()
    on_right.start()
    left_second.wait_recv()
    on_left.start()
    right_second.wait_recv()
    left_first.wait_recv()
    on_right.wait_recv()
    on_left.wait_recv()
    keep.wait()
    for copy in (right_first, left_second, right_second, left_first, on_right, on_left):
        copy.wait_send()


def head_gather(block):
    rows, width = block.shape
    return pl.pallas_call(
        head_gather_kernel,
        out_shape=jax.ShapeDtypeStruct((4, rows, width), block.dtype),
        in_specs=[pl.BlockSpec(memory_space=pltpu.VMEM)],
        out_specs=pl.BlockSpec(memory_space=pltpu.VMEM),
        scratch_shapes=[
            pltpu.SemaphoreType.DMA((6,)),
            pltpu.SemaphoreType.DMA((6,)),
            pltpu.SemaphoreType.DMA,
        ],
        compiler_params=pltpu.CompilerParams(collective_id=0, has_side_effects=True),
    )(block)


def attend_kernel(length_ref, q_ref, kv_ref, o_ref, buf, max_ref, sum_ref, acc_ref, send_sem, recv_sem):
    seq = lax.axis_index("seq")
    half = lax.div(seq, PLANE)
    y = lax.rem(lax.div(seq, 2), 4)
    core = lax.rem(seq, 2)
    base = half * PLANE
    right = {"seq": base + lax.rem(y + 1, 4) * 2 + core}
    left = {"seq": base + lax.rem(y + 3, 4) * 2 + core}
    partner = {"seq": base + y * 2 + (1 - core)}
    rows = kv_ref.shape[0]
    heads = q_ref.shape[1] // HEAD
    first, second = pl.ds(0, rows // 2), pl.ds(rows // 2, rows // 2)
    length = length_ref[0]

    barrier([left, right, partner])
    right_first = remote(kv_ref.at[first], buf.at[3, 0, first], send_sem, recv_sem, 0, right)
    left_second = remote(kv_ref.at[second], buf.at[1, 0, second], send_sem, recv_sem, 1, left)
    right_second = remote(kv_ref.at[second], buf.at[3, 0, second], send_sem, recv_sem, 2, right)
    left_first = remote(kv_ref.at[first], buf.at[1, 0, first], send_sem, recv_sem, 3, left)
    across_own = remote(kv_ref, buf.at[0, 1], send_sem, recv_sem, 4, partner)
    on_right = remote(buf.at[3, 0, first], buf.at[2, 0, first], send_sem, recv_sem, 5, right)
    on_left = remote(buf.at[1, 0, second], buf.at[2, 0, second], send_sem, recv_sem, 6, left)
    across_left = remote(buf.at[3, 0], buf.at[3, 1], send_sem, recv_sem, 7, partner)
    across_right = remote(buf.at[1, 0], buf.at[1, 1], send_sem, recv_sem, 8, partner)
    across_first = remote(buf.at[2, 0, first], buf.at[2, 1, first], send_sem, recv_sem, 9, partner)
    across_second = remote(buf.at[2, 0, second], buf.at[2, 1, second], send_sem, recv_sem, 10, partner)

    def attend_shard(shard, distance, other_core):
        source = lax.rem(y + distance, 4) * 2 + lax.rem(core + other_core, 2)
        row = lax.broadcasted_iota(jnp.int32, (1, rows), 1)
        slot = jnp.bitwise_and(jnp.right_shift(row, 6), 1)
        which = jnp.bitwise_xor(slot, half)
        position = which * 2048 + source * 256 + jnp.right_shift(row, 7) * 64 + jnp.bitwise_and(row, 63)
        valid = position < length

        def one_head(h, carry):
            k_columns = pl.ds(pl.multiple_of(h * HEAD, HEAD), HEAD)
            v_columns = pl.ds(pl.multiple_of((heads + h) * HEAD, HEAD), HEAD)
            scores = lax.dot_general(
                q_ref[:, k_columns],
                shard[:, k_columns],
                (((1,), (1,)), ((), ())),
                preferred_element_type=jnp.float32,
            )
            scores = jnp.where(valid, scores * EXP2_SCALE, -1e30)
            old_max = max_ref[h]
            new_max = jnp.maximum(old_max, jnp.max(scores, axis=1, keepdims=True))
            rescale = jnp.exp2(old_max - new_max)
            weights = jnp.exp2(scores - new_max[:, :1])
            max_ref[h] = new_max
            sum_ref[h] = sum_ref[h] * rescale + jnp.sum(weights, axis=1, keepdims=True)
            acc_ref[h] = acc_ref[h] * rescale + jnp.dot(
                weights.astype(jnp.bfloat16), shard[:, v_columns], preferred_element_type=jnp.float32
            )
            return carry

        lax.fori_loop(0, heads, one_head, 0)

    right_first.start()
    left_second.start()
    right_second.start()
    left_first.start()
    across_own.start()
    max_ref[...] = jnp.full_like(max_ref, -1e30)
    sum_ref[...] = jnp.zeros_like(sum_ref)
    acc_ref[...] = jnp.zeros_like(acc_ref)
    attend_shard(kv_ref, 0, 0)
    right_first.wait_recv()
    on_right.start()
    left_second.wait_recv()
    on_left.start()
    across_own.wait_recv()
    attend_shard(buf.at[0, 1], 0, 1)
    right_second.wait_recv()
    across_left.start()
    left_first.wait_recv()
    across_right.start()
    attend_shard(buf.at[3, 0], 3, 0)
    attend_shard(buf.at[1, 0], 1, 0)
    on_right.wait_recv()
    across_first.start()
    on_left.wait_recv()
    across_second.start()
    across_left.wait_recv()
    attend_shard(buf.at[3, 1], 3, 1)
    across_right.wait_recv()
    attend_shard(buf.at[1, 1], 1, 1)
    attend_shard(buf.at[2, 0], 2, 0)
    across_first.wait_recv()
    across_second.wait_recv()
    attend_shard(buf.at[2, 1], 2, 1)
    for h in range(heads):
        o_ref[:, h * HEAD : (h + 1) * HEAD] = (acc_ref[h] / sum_ref[h]).astype(o_ref.dtype)
    for copy in (
        right_first,
        left_second,
        right_second,
        left_first,
        across_own,
        on_right,
        on_left,
        across_left,
        across_right,
        across_first,
        across_second,
    ):
        copy.wait_send()


def attend(length, queries, key_value):
    rows, width = queries.shape
    heads = width // HEAD
    stats = pltpu.VMEM((heads, rows, HEAD), jnp.float32)
    return pl.pallas_call(
        attend_kernel,
        in_specs=[
            pl.BlockSpec(memory_space=pltpu.SMEM),
            pl.BlockSpec(memory_space=pltpu.VMEM),
            pl.BlockSpec(memory_space=pltpu.VMEM),
        ],
        out_specs=pl.BlockSpec(memory_space=pltpu.VMEM),
        out_shape=jax.ShapeDtypeStruct((rows, width), jnp.bfloat16),
        scratch_shapes=[
            pltpu.VMEM((4, 2) + key_value.shape, key_value.dtype),
            stats,
            stats,
            stats,
            pltpu.SemaphoreType.DMA((11,)),
            pltpu.SemaphoreType.DMA((11,)),
        ],
        compiler_params=pltpu.CompilerParams(collective_id=1, has_side_effects=True),
    )(length, queries, key_value)


def finish_kernel(partial_ref, state_ref, gate_ref, out_ref, landed, updated, send_sem, recv_sem):
    me = lax.axis_index("head")
    position = lax.axis_index("segment")
    rows = state_ref.shape[0]
    ahead = [lax.rem(me + distance, 4) for distance in (1, 2, 3)]
    following = {"segment": lax.rem(position + 1, 8)}
    preceding = {"segment": lax.rem(position + 7, 8)}
    barrier([{"head": peer} for peer in ahead] + [preceding])
    copies = []
    for index in (1, 0, 2):
        piece = pl.ds(pl.multiple_of(ahead[index] * rows, rows), rows)
        copies.append(
            remote(partial_ref.at[piece], landed.at[index], send_sem, recv_sem, index, {"head": ahead[index]})
        )
        copies[-1].start()
    for copy in copies:
        copy.wait_recv()
    mine = pl.ds(pl.multiple_of(me * rows, rows), rows)
    branch = partial_ref[mine, :].astype(jnp.float32)
    for index in range(3):
        branch = branch + landed[index].astype(jnp.float32)
    updated[...] = (state_ref[...].astype(jnp.float32) + gate_ref[...] * branch).astype(updated.dtype)
    onward = remote(updated, out_ref, send_sem, recv_sem, 3, following)
    onward.start()
    for copy in copies:
        copy.wait_send()
    onward.wait()


def finish(partial, state, gate_row):
    vmem = pl.BlockSpec(memory_space=pltpu.VMEM)
    return pl.pallas_call(
        finish_kernel,
        in_specs=[vmem, vmem, vmem],
        out_specs=vmem,
        out_shape=jax.ShapeDtypeStruct(state.shape, state.dtype),
        scratch_shapes=[
            pltpu.VMEM((3,) + state.shape, partial.dtype),
            pltpu.VMEM(state.shape, state.dtype),
            pltpu.SemaphoreType.DMA((4,)),
            pltpu.SemaphoreType.DMA((4,)),
        ],
        compiler_params=pltpu.CompilerParams(collective_id=2, has_side_effects=True),
    )(partial, state, gate_row)


def per_device(tokens, lengths, modulation, gate_gain, w_qkv, w_out):
    segment_count = lax.axis_size("segment")
    seq_count = lax.axis_size("seq")
    position = lax.axis_index("segment")
    shift_scale = modulation[0].astype(jnp.float32)
    gate_row = gate_gain[0].astype(jnp.float32)
    model_width = w_qkv.shape[1]
    local_width = w_qkv.shape[3]
    flat_qkv = w_qkv[0].reshape(model_width, 3 * local_width)
    out_rows = w_out[0]
    own = tokens[0]
    for tick_index in range(TICKS):
        micro_index = (position - tick_index) % segment_count
        length = lax.dynamic_index_in_dim(lengths, micro_index, 0, keepdims=False)
        other = lax.ppermute(own, "seq", [(i, (i + PLANE) % seq_count) for i in range(seq_count)])
        both = jnp.concatenate([own, other], axis=0).astype(jnp.float32)
        normed = (layer_norm(both) * (1.0 + shift_scale[1]) + shift_scale[0]).astype(jnp.bfloat16)
        rows = head_gather(normed).reshape(-1, model_width)
        projected = jnp.dot(rows, flat_qkv, preferred_element_type=jnp.float32).astype(jnp.bfloat16)
        tile = own.shape[0]
        queries = projected[:, :local_width].reshape(-1, 2, tile, local_width)[:, 0]
        queries = queries.reshape(-1, local_width)
        attended = attend(length[None], queries, projected[:, local_width:])
        partial = jnp.dot(attended, out_rows, preferred_element_type=jnp.float32).astype(jnp.bfloat16)
        own = finish(partial, own, gate_row[None])
    return own[None]


def solution(mesh):
    return jax.shard_map(
        per_device,
        mesh=mesh,
        in_specs=(
            P("segment", ("seq", "head"), None),
            P(),
            P("segment", None, None),
            P("segment", None),
            P("segment", None, None, "head"),
            P("segment", "head", None),
        ),
        out_specs=P("segment", ("seq", "head"), None),
        check_vma=False,
    )
```

```python
import math

import jax
import jax.numpy as jnp
from jax import lax
from jax.experimental import pallas as pl
from jax.experimental.pallas import tpu as pltpu
from jax.sharding import PartitionSpec as P

HEAD = 128
TICKS = 2
PLANE = 8
MESH = pl.DeviceIdType.MESH
EXP2_SCALE = HEAD ** (-0.5) * math.log2(math.e)


def layer_norm(values):
    row_mean = jnp.mean(values, axis=-1, keepdims=True)
    centered = values - row_mean
    row_var = jnp.mean(centered * centered, axis=-1, keepdims=True)
    return centered / jnp.sqrt(row_var + 1e-06)


def barrier(peers):
    sem = pltpu.get_barrier_semaphore()
    for peer in peers:
        pl.semaphore_signal(sem, inc=1, device_id=peer, device_id_type=MESH)
    pl.semaphore_wait(sem, len(peers))


def remote(src, dst, send_sem, recv_sem, index, peer):
    return pltpu.make_async_remote_copy(
        src_ref=src,
        dst_ref=dst,
        send_sem=send_sem.at[index],
        recv_sem=recv_sem.at[index],
        device_id=peer,
        device_id_type=MESH,
    )


def ring_copies(source, target, here, behind, left, right, rows, send_sem, recv_sem, index):
    first, second = pl.ds(0, rows // 2), pl.ds(rows // 2, rows // 2)
    return {
        "right_first": remote(source.at[first], here(1).at[first], send_sem, recv_sem, index, right),
        "left_second": remote(source.at[second], here(3).at[second], send_sem, recv_sem, index + 1, left),
        "right_second": remote(source.at[second], here(1).at[second], send_sem, recv_sem, index + 2, right),
        "left_first": remote(source.at[first], here(3).at[first], send_sem, recv_sem, index + 3, left),
        "on_right": remote(behind(1).at[first], target(1).at[first], send_sem, recv_sem, index + 4, right),
        "on_left": remote(behind(3).at[second], target(3).at[second], send_sem, recv_sem, index + 5, left),
    }


FIRST_HOPS = ("right_first", "left_second", "right_second", "left_first")


def attend_kernel(
    length_ref, normed_ref, w_ref, o_ref, rows_ref, q_ref, kv_ref, buf, max_ref, sum_ref, acc_ref,
    send_sem, recv_sem, local_sem,
):
    seq = lax.axis_index("seq")
    me = lax.axis_index("head")
    half = lax.div(seq, PLANE)
    y = lax.rem(lax.div(seq, 2), 4)
    core = lax.rem(seq, 2)
    base = half * PLANE
    y_right = {"seq": base + lax.rem(y + 1, 4) * 2 + core}
    y_left = {"seq": base + lax.rem(y + 3, 4) * 2 + core}
    partner = {"seq": base + y * 2 + (1 - core)}
    far = {"seq": lax.rem(seq + PLANE, 2 * PLANE)}
    x_right_at, x_left_at = lax.rem(me + 1, 4), lax.rem(me + 3, 4)
    x_right, x_left = {"head": x_right_at}, {"head": x_left_at}
    tile = normed_ref.shape[0]
    rows = kv_ref.shape[1]
    width = q_ref.shape[1]
    heads = width // HEAD
    length = length_ref[0]

    barrier([x_left, x_right, y_left, y_right, partner, far])

    def x_copies(slot, source, index):
        def own(d):
            return rows_ref.at[slot, me]

        def neighbour(d):
            return rows_ref.at[slot, x_left_at] if d == 1 else rows_ref.at[slot, x_right_at]

        return ring_copies(source, neighbour, own, neighbour, x_left, x_right, tile, send_sem, recv_sem, index)

    def y_copies(slot, index):
        def landing(d):
            return buf.at[d, 0, slot]

        def opposite(d):
            return buf.at[2, 0, slot]

        copies = ring_copies(
            kv_ref.at[slot], opposite, landing, landing, y_left, y_right, rows, send_sem, recv_sem, index
        )
        first, second = pl.ds(0, rows // 2), pl.ds(rows // 2, rows // 2)
        across = {
            "across_own": (kv_ref.at[slot], buf.at[0, 1, slot]),
            "across_left": (buf.at[1, 0, slot], buf.at[1, 1, slot]),
            "across_right": (buf.at[3, 0, slot], buf.at[3, 1, slot]),
            "across_first": (buf.at[2, 0, slot, first], buf.at[2, 1, slot, first]),
            "across_second": (buf.at[2, 0, slot, second], buf.at[2, 1, slot, second]),
        }
        for offset, (name, (source, target)) in enumerate(across.items()):
            copies[name] = remote(source, target, send_sem, recv_sem, index + 6 + offset, partner)
        return copies

    swap = remote(normed_ref, rows_ref.at[1, me], send_sem, recv_sem, 0, far)
    keep = pltpu.make_async_copy(normed_ref, rows_ref.at[0, me], local_sem)
    x_own = x_copies(0, normed_ref, 1)
    x_far = x_copies(1, rows_ref.at[1, me], 7)
    y_own = y_copies(0, 13)
    y_far = y_copies(1, 24)

    def send_first(copies):
        for name in FIRST_HOPS:
            copies[name].start()

    def pass_on(copies):
        copies["right_first"].wait_recv()
        copies["on_right"].start()
        copies["left_second"].wait_recv()
        copies["on_left"].start()

    def rest_of_x(copies):
        for name in ("right_second", "left_first", "on_right", "on_left"):
            copies[name].wait_recv()

    def neighbours_across(copies):
        copies["right_second"].wait_recv()
        copies["across_left"].start()
        copies["left_first"].wait_recv()
        copies["across_right"].start()

    def opposite_across(copies):
        copies["on_right"].wait_recv()
        copies["across_first"].start()
        copies["on_left"].wait_recv()
        copies["across_second"].start()

    def project(slot, group):
        block = rows_ref[slot].reshape(rows, rows_ref.shape[3])
        return jnp.dot(block, w_ref[group], preferred_element_type=jnp.float32).astype(jnp.bfloat16)

    def project_kv(slot):
        def one(part, carry):
            kv_ref[slot, :, pl.ds(pl.multiple_of(part * width, HEAD), width)] = project(slot, part + 1)
            return carry

        lax.fori_loop(0, 2, one, 0)

    def attend_shard(shard, behind, other_core, slot):
        source = lax.rem(y + 4 - behind, 4) * 2 + lax.rem(core + other_core, 2)
        which = half if slot == 0 else 1 - half
        position = lax.broadcasted_iota(jnp.int32, (1, rows), 1) + (which * PLANE + source) * rows
        valid = position < length

        def one_head(h, carry):
            k_columns = pl.ds(pl.multiple_of(h * HEAD, HEAD), HEAD)
            v_columns = pl.ds(pl.multiple_of((heads + h) * HEAD, HEAD), HEAD)
            scores = lax.dot_general(
                q_ref[:, k_columns],
                shard[:, k_columns],
                (((1,), (1,)), ((), ())),
                preferred_element_type=jnp.float32,
            )
            scores = jnp.where(valid, scores * EXP2_SCALE, -1e30)
            old_max = max_ref[h]
            new_max = jnp.maximum(old_max, jnp.max(scores, axis=1, keepdims=True))
            rescale = jnp.exp2(old_max - new_max)
            weights = jnp.exp2(scores - new_max[:, :1])
            max_ref[h] = new_max
            sum_ref[h] = sum_ref[h] * rescale + jnp.sum(weights, axis=1, keepdims=True)
            acc_ref[h] = acc_ref[h] * rescale + jnp.dot(
                weights.astype(jnp.bfloat16), shard[:, v_columns], preferred_element_type=jnp.float32
            )
            return carry

        lax.fori_loop(0, heads, one_head, 0)

    def attend_buf(behind, other_core, slot):
        attend_shard(buf.at[behind, other_core, slot], behind, other_core, slot)

    swap.start()
    send_first(x_own)
    keep.start()
    max_ref[...] = jnp.full_like(max_ref, -1e30)
    sum_ref[...] = jnp.zeros_like(sum_ref)
    acc_ref[...] = jnp.zeros_like(acc_ref)
    pass_on(x_own)
    rest_of_x(x_own)
    keep.wait()
    project_kv(0)
    send_first(y_own)
    y_own["across_own"].start()
    q_ref[...] = project(0, 0)
    attend_shard(kv_ref.at[0], 0, 0, 0)
    pass_on(y_own)
    swap.wait_recv()
    send_first(x_far)
    neighbours_across(y_own)
    y_own["across_own"].wait_recv()
    attend_buf(0, 1, 0)
    pass_on(x_far)
    attend_buf(1, 0, 0)
    attend_buf(3, 0, 0)
    opposite_across(y_own)
    rest_of_x(x_far)
    project_kv(1)
    send_first(y_far)
    y_far["across_own"].start()
    attend_shard(kv_ref.at[1], 0, 0, 1)
    y_own["across_left"].wait_recv()
    attend_buf(1, 1, 0)
    pass_on(y_far)
    y_own["across_right"].wait_recv()
    attend_buf(3, 1, 0)
    attend_buf(2, 0, 0)
    neighbours_across(y_far)
    y_own["across_first"].wait_recv()
    y_own["across_second"].wait_recv()
    attend_buf(2, 1, 0)
    y_far["across_own"].wait_recv()
    attend_buf(0, 1, 1)
    attend_buf(1, 0, 1)
    opposite_across(y_far)
    attend_buf(3, 0, 1)
    y_far["across_left"].wait_recv()
    attend_buf(1, 1, 1)
    y_far["across_right"].wait_recv()
    attend_buf(3, 1, 1)
    attend_buf(2, 0, 1)
    y_far["across_first"].wait_recv()
    y_far["across_second"].wait_recv()
    attend_buf(2, 1, 1)
    for h in range(heads):
        o_ref[:, h * HEAD : (h + 1) * HEAD] = (acc_ref[h] / sum_ref[h]).astype(o_ref.dtype)
    swap.wait_send()
    for copies in (x_own, x_far, y_own, y_far):
        for copy in copies.values():
            copy.wait_send()


def attend(length, normed, weights):
    tile, model_width = normed.shape
    width = weights.shape[2]
    rows = 4 * tile
    vmem = pl.BlockSpec(memory_space=pltpu.VMEM)
    stats = pltpu.VMEM((width // HEAD, rows, HEAD), jnp.float32)
    return pl.pallas_call(
        attend_kernel,
        in_specs=[pl.BlockSpec(memory_space=pltpu.SMEM), vmem, vmem],
        out_specs=vmem,
        out_shape=jax.ShapeDtypeStruct((rows, width), jnp.bfloat16),
        scratch_shapes=[
            pltpu.VMEM((2, 4, tile, model_width), normed.dtype),
            pltpu.VMEM((rows, width), normed.dtype),
            pltpu.VMEM((2, rows, 2 * width), normed.dtype),
            pltpu.VMEM((4, 2, 2, rows, 2 * width), normed.dtype),
            stats,
            stats,
            stats,
            pltpu.SemaphoreType.DMA((35,)),
            pltpu.SemaphoreType.DMA((35,)),
            pltpu.SemaphoreType.DMA,
        ],
        compiler_params=pltpu.CompilerParams(collective_id=1, has_side_effects=True),
    )(length, normed, weights)


def finish_kernel(partial_ref, state_ref, gate_ref, out_ref, landed, updated, send_sem, recv_sem):
    me = lax.axis_index("head")
    position = lax.axis_index("segment")
    rows = state_ref.shape[0]
    ahead = [lax.rem(me + distance, 4) for distance in (1, 2, 3)]
    following = {"segment": lax.rem(position + 1, 8)}
    preceding = {"segment": lax.rem(position + 7, 8)}
    barrier([{"head": peer} for peer in ahead] + [preceding])
    copies = []
    for index in (1, 0, 2):
        piece = pl.ds(pl.multiple_of(ahead[index] * rows, rows), rows)
        copies.append(
            remote(partial_ref.at[piece], landed.at[index], send_sem, recv_sem, index, {"head": ahead[index]})
        )
        copies[-1].start()
    for copy in copies:
        copy.wait_recv()
    mine = pl.ds(pl.multiple_of(me * rows, rows), rows)
    branch = partial_ref[mine, :].astype(jnp.float32)
    for index in range(3):
        branch = branch + landed[index].astype(jnp.float32)
    updated[...] = (state_ref[...].astype(jnp.float32) + gate_ref[...] * branch).astype(updated.dtype)
    onward = remote(updated, out_ref, send_sem, recv_sem, 3, following)
    onward.start()
    for copy in copies:
        copy.wait_send()
    onward.wait()


def finish(partial, state, gate_row):
    vmem = pl.BlockSpec(memory_space=pltpu.VMEM)
    return pl.pallas_call(
        finish_kernel,
        in_specs=[vmem, vmem, vmem],
        out_specs=vmem,
        out_shape=jax.ShapeDtypeStruct(state.shape, state.dtype),
        scratch_shapes=[
            pltpu.VMEM((3,) + state.shape, partial.dtype),
            pltpu.VMEM(state.shape, state.dtype),
            pltpu.SemaphoreType.DMA((4,)),
            pltpu.SemaphoreType.DMA((4,)),
        ],
        compiler_params=pltpu.CompilerParams(collective_id=2, has_side_effects=True),
    )(partial, state, gate_row)


def per_device(tokens, lengths, modulation, gate_gain, w_qkv, w_out):
    segment_count = lax.axis_size("segment")
    position = lax.axis_index("segment")
    shift_scale = modulation[0].astype(jnp.float32)
    gate_row = gate_gain[0].astype(jnp.float32)
    parts_qkv = jnp.transpose(w_qkv[0], (1, 0, 2))
    out_rows = w_out[0]
    own = tokens[0]
    for tick_index in range(TICKS):
        micro_index = (position - tick_index) % segment_count
        length = lax.dynamic_index_in_dim(lengths, micro_index, 0, keepdims=False)
        values = own.astype(jnp.float32)
        normed = (layer_norm(values) * (1.0 + shift_scale[1]) + shift_scale[0]).astype(jnp.bfloat16)
        attended = attend(length[None], normed, parts_qkv)
        partial = jnp.dot(attended, out_rows, preferred_element_type=jnp.float32).astype(jnp.bfloat16)
        own = finish(partial, own, gate_row[None])
    return own[None]


def solution(mesh):
    return jax.shard_map(
        per_device,
        mesh=mesh,
        in_specs=(
            P("segment", ("seq", "head"), None),
            P(),
            P("segment", None, None),
            P("segment", None),
            P("segment", None, None, "head"),
            P("segment", "head", None),
        ),
        out_specs=P("segment", ("seq", "head"), None),
        check_vma=False,
    )
```

```python
import math

import jax
import jax.numpy as jnp
from jax import lax
from jax.experimental import pallas as pl
from jax.experimental.pallas import tpu as pltpu
from jax.sharding import PartitionSpec as P

HEAD = 128
TICKS = 2
PLANE = 8
MESH = pl.DeviceIdType.MESH
EXP2_SCALE = HEAD ** (-0.5) * math.log2(math.e)


def layer_norm(values):
    row_mean = jnp.mean(values, axis=-1, keepdims=True)
    centered = values - row_mean
    row_var = jnp.mean(centered * centered, axis=-1, keepdims=True)
    return centered / jnp.sqrt(row_var + 1e-06)


def remote(src, dst, send_sem, recv_sem, index, peer):
    return pltpu.make_async_remote_copy(
        src_ref=src,
        dst_ref=dst,
        send_sem=send_sem.at[index],
        recv_sem=recv_sem.at[index],
        device_id=peer,
        device_id_type=MESH,
    )


def ring_copies(source, target, here, behind, left, right, rows, send_sem, recv_sem, index):
    first, second = pl.ds(0, rows // 2), pl.ds(rows // 2, rows // 2)
    return {
        "right_first": remote(source.at[first], here(1).at[first], send_sem, recv_sem, index, right),
        "left_second": remote(source.at[second], here(3).at[second], send_sem, recv_sem, index + 1, left),
        "right_second": remote(source.at[second], here(1).at[second], send_sem, recv_sem, index + 2, right),
        "left_first": remote(source.at[first], here(3).at[first], send_sem, recv_sem, index + 3, left),
        "on_right": remote(behind(1).at[first], target(1).at[first], send_sem, recv_sem, index + 4, right),
        "on_left": remote(behind(3).at[second], target(3).at[second], send_sem, recv_sem, index + 5, left),
    }


FIRST_HOPS = ("right_first", "left_second", "right_second", "left_first")


def layer_kernel(
    length_ref, state_ref, modulation_ref, gate_ref, w_ref, out_w_ref, o_ref,
    rows_ref, q_ref, kv_ref, buf, max_ref, sum_ref, acc_ref, attended_ref, part_ref, relay_ref,
    landed_ref, updated_ref, send_sem, recv_sem,
):
    seq = lax.axis_index("seq")
    me = lax.axis_index("head")
    half = lax.div(seq, PLANE)
    y = lax.rem(lax.div(seq, 2), 4)
    core = lax.rem(seq, 2)
    base = half * PLANE
    y_right = {"seq": base + lax.rem(y + 1, 4) * 2 + core}
    y_left = {"seq": base + lax.rem(y + 3, 4) * 2 + core}
    partner = {"seq": base + y * 2 + (1 - core)}
    far = {"seq": lax.rem(seq + PLANE, 2 * PLANE)}
    x_right_at, x_left_at = lax.rem(me + 1, 4), lax.rem(me + 3, 4)
    x_right, x_left = {"head": x_right_at}, {"head": x_left_at}
    x_opposite_at = lax.rem(me + 2, 4)
    position_at = lax.axis_index("segment")
    following = {"segment": lax.rem(position_at + 1, 8)}
    preceding = {"segment": lax.rem(position_at + 7, 8)}
    tile = state_ref.shape[0]
    rows = kv_ref.shape[1]
    width = q_ref.shape[1]
    heads = width // HEAD
    length = length_ref[0]

    peers = [x_left, x_right, y_left, y_right, partner, far, preceding]
    entry = pltpu.get_barrier_semaphore()
    for peer in peers:
        pl.semaphore_signal(entry, inc=1, device_id=peer, device_id_type=MESH)
    values = state_ref[...].astype(jnp.float32)
    shift = modulation_ref[0:1, :].astype(jnp.float32)
    scale = modulation_ref[1:2, :].astype(jnp.float32)
    rows_ref[0, me] = (layer_norm(values) * (1.0 + scale) + shift).astype(rows_ref.dtype)
    max_ref[...] = jnp.full_like(max_ref, -1e30)
    sum_ref[...] = jnp.zeros_like(sum_ref)
    acc_ref[...] = jnp.zeros_like(acc_ref)
    pl.semaphore_wait(entry, len(peers))

    def x_copies(slot, source, index):
        def own(d):
            return rows_ref.at[slot, me]

        def neighbour(d):
            return rows_ref.at[slot, x_left_at] if d == 1 else rows_ref.at[slot, x_right_at]

        return ring_copies(source, neighbour, own, neighbour, x_left, x_right, tile, send_sem, recv_sem, index)

    def y_copies(slot, index):
        def landing(d):
            return buf.at[d, 0, slot]

        def opposite(d):
            return buf.at[2, 0, slot]

        copies = ring_copies(
            kv_ref.at[slot], opposite, landing, landing, y_left, y_right, rows, send_sem, recv_sem, index
        )
        first, second = pl.ds(0, rows // 2), pl.ds(rows // 2, rows // 2)
        across = {
            "across_own": (kv_ref.at[slot], buf.at[0, 1, slot]),
            "across_left": (buf.at[1, 0, slot], buf.at[1, 1, slot]),
            "across_right": (buf.at[3, 0, slot], buf.at[3, 1, slot]),
            "across_first": (buf.at[2, 0, slot, first], buf.at[2, 1, slot, first]),
            "across_second": (buf.at[2, 0, slot, second], buf.at[2, 1, slot, second]),
        }
        for offset, (name, (source, target)) in enumerate(across.items()):
            copies[name] = remote(source, target, send_sem, recv_sem, index + 6 + offset, partner)
        return copies

    top, bottom = pl.ds(0, tile // 2), pl.ds(tile // 2, tile // 2)
    swap_top = remote(rows_ref.at[0, me, top], rows_ref.at[1, me, top], send_sem, recv_sem, 0, far)
    swap_bottom = remote(rows_ref.at[0, me, bottom], rows_ref.at[1, me, bottom], send_sem, recv_sem, 35, far)
    x_own = x_copies(0, rows_ref.at[0, me], 1)
    x_far = x_copies(1, rows_ref.at[1, me], 7)
    y_own = y_copies(0, 13)
    y_far = y_copies(1, 24)

    def send_first(copies):
        for name in FIRST_HOPS:
            copies[name].start()

    def pass_on(copies):
        copies["right_first"].wait_recv()
        copies["on_right"].start()
        copies["left_second"].wait_recv()
        copies["on_left"].start()

    def rest_of_x(copies):
        for name in ("right_second", "left_first", "on_right", "on_left"):
            copies[name].wait_recv()

    def neighbours_across(copies):
        copies["right_second"].wait_recv()
        copies["across_left"].start()
        copies["left_first"].wait_recv()
        copies["across_right"].start()

    def opposite_across(copies):
        copies["on_right"].wait_recv()
        copies["across_first"].start()
        copies["on_left"].wait_recv()
        copies["across_second"].start()

    def project(slot, group):
        block = rows_ref[slot].reshape(rows, rows_ref.shape[3])
        return jnp.dot(block, w_ref[group], preferred_element_type=jnp.float32).astype(jnp.bfloat16)

    def project_kv(slot):
        def one(part, carry):
            kv_ref[slot, :, pl.ds(pl.multiple_of(part * width, HEAD), width)] = project(slot, part + 1)
            return carry

        lax.fori_loop(0, 2, one, 0)

    def attend_shard(shard, behind, other_core, slot):
        source = lax.rem(y + 4 - behind, 4) * 2 + lax.rem(core + other_core, 2)
        which = half if slot == 0 else 1 - half
        position = lax.broadcasted_iota(jnp.int32, (1, rows), 1) + (which * PLANE + source) * rows
        valid = position < length

        def one_head(h, carry):
            k_columns = pl.ds(pl.multiple_of(h * HEAD, HEAD), HEAD)
            v_columns = pl.ds(pl.multiple_of((heads + h) * HEAD, HEAD), HEAD)
            scores = lax.dot_general(
                q_ref[:, k_columns],
                shard[:, k_columns],
                (((1,), (1,)), ((), ())),
                preferred_element_type=jnp.float32,
            )
            scores = jnp.where(valid, scores * EXP2_SCALE, -1e30)
            old_max = max_ref[h]
            new_max = jnp.maximum(old_max, jnp.max(scores, axis=1, keepdims=True))
            rescale = jnp.exp2(old_max - new_max)
            weights = jnp.exp2(scores - new_max[:, :1])
            max_ref[h] = new_max
            sum_ref[h] = sum_ref[h] * rescale + jnp.sum(weights, axis=1, keepdims=True)
            acc_ref[h] = acc_ref[h] * rescale + jnp.dot(
                weights.astype(jnp.bfloat16), shard[:, v_columns], preferred_element_type=jnp.float32
            )
            return carry

        lax.fori_loop(0, heads, one_head, 0)

    def attend_buf(behind, other_core, slot):
        attend_shard(buf.at[behind, other_core, slot], behind, other_core, slot)

    swap_top.start()
    swap_bottom.start()
    send_first(x_own)
    pass_on(x_own)
    rest_of_x(x_own)
    project_kv(0)
    send_first(y_own)
    y_own["across_own"].start()
    q_ref[...] = project(0, 0)
    attend_shard(kv_ref.at[0], 0, 0, 0)
    pass_on(y_own)
    swap_top.wait_recv()
    x_far["right_first"].start()
    x_far["left_first"].start()
    neighbours_across(y_own)
    swap_bottom.wait_recv()
    x_far["left_second"].start()
    x_far["right_second"].start()
    y_own["across_own"].wait_recv()
    attend_buf(0, 1, 0)
    pass_on(x_far)
    attend_buf(1, 0, 0)
    attend_buf(3, 0, 0)
    opposite_across(y_own)
    rest_of_x(x_far)
    project_kv(1)
    send_first(y_far)
    y_far["across_own"].start()
    attend_shard(kv_ref.at[1], 0, 0, 1)
    y_own["across_left"].wait_recv()
    attend_buf(1, 1, 0)
    pass_on(y_far)
    y_own["across_right"].wait_recv()
    attend_buf(3, 1, 0)
    attend_buf(2, 0, 0)
    neighbours_across(y_far)
    y_own["across_first"].wait_recv()
    y_own["across_second"].wait_recv()
    attend_buf(2, 1, 0)
    y_far["across_own"].wait_recv()
    attend_buf(0, 1, 1)
    attend_buf(1, 0, 1)
    opposite_across(y_far)
    attend_buf(3, 0, 1)
    y_far["across_left"].wait_recv()
    attend_buf(1, 1, 1)
    y_far["across_right"].wait_recv()
    attend_buf(3, 1, 1)
    attend_buf(2, 0, 1)
    y_far["across_first"].wait_recv()
    y_far["across_second"].wait_recv()
    attend_buf(2, 1, 1)
    for h in range(heads):
        attended_ref[:, h * HEAD : (h + 1) * HEAD] = (acc_ref[h] / sum_ref[h]).astype(attended_ref.dtype)

    def branch_of(device):
        block = attended_ref[pl.ds(pl.multiple_of(device * tile, tile), tile), :]
        return jnp.dot(block, out_w_ref[...], preferred_element_type=jnp.float32)

    to_right = remote(part_ref.at[0, top], relay_ref.at[0], send_sem, recv_sem, 36, x_right)
    to_left = remote(part_ref.at[0, bottom], relay_ref.at[1], send_sem, recv_sem, 37, x_left)
    plain_right = remote(part_ref.at[1, bottom], landed_ref.at[0, bottom], send_sem, recv_sem, 38, x_right)
    plain_left = remote(part_ref.at[2, top], landed_ref.at[1, top], send_sem, recv_sem, 39, x_left)
    sum_right = remote(part_ref.at[1, top], landed_ref.at[0, top], send_sem, recv_sem, 40, x_right)
    sum_left = remote(part_ref.at[2, bottom], landed_ref.at[1, bottom], send_sem, recv_sem, 41, x_left)
    onward = remote(updated_ref, o_ref, send_sem, recv_sem, 42, following)
    part_ref[0] = branch_of(x_opposite_at).astype(part_ref.dtype)
    to_right.start()
    to_left.start()
    part_ref[1] = branch_of(x_right_at).astype(part_ref.dtype)
    plain_right.start()
    part_ref[2] = branch_of(x_left_at).astype(part_ref.dtype)
    plain_left.start()
    to_right.wait_recv()
    part_ref[1, top, :] = (
        part_ref[1, top, :].astype(jnp.float32) + relay_ref[0].astype(jnp.float32)
    ).astype(part_ref.dtype)
    sum_right.start()
    to_left.wait_recv()
    part_ref[2, bottom, :] = (
        part_ref[2, bottom, :].astype(jnp.float32) + relay_ref[1].astype(jnp.float32)
    ).astype(part_ref.dtype)
    sum_left.start()
    branch = branch_of(me)
    for copy in (plain_right, plain_left, sum_right, sum_left):
        copy.wait_recv()
    branch = branch + landed_ref[0].astype(jnp.float32) + landed_ref[1].astype(jnp.float32)
    updated_ref[...] = (
        state_ref[...].astype(jnp.float32) + gate_ref[...].astype(jnp.float32) * branch
    ).astype(updated_ref.dtype)
    onward.start()
    for copy in (swap_top, swap_bottom, to_right, to_left, plain_right, plain_left, sum_right, sum_left):
        copy.wait_send()
    for copies in (x_own, x_far, y_own, y_far):
        for copy in copies.values():
            copy.wait_send()
    onward.wait()


def layer(length, state, modulation, gate, weights, out_weights):
    tile, model_width = state.shape
    width = weights.shape[2]
    rows = 4 * tile
    kind = state.dtype
    vmem = pl.BlockSpec(memory_space=pltpu.VMEM)
    stats = pltpu.VMEM((width // HEAD, rows, HEAD), jnp.float32)
    return pl.pallas_call(
        layer_kernel,
        in_specs=[pl.BlockSpec(memory_space=pltpu.SMEM), vmem, vmem, vmem, vmem, vmem],
        out_specs=vmem,
        out_shape=jax.ShapeDtypeStruct(state.shape, kind),
        scratch_shapes=[
            pltpu.VMEM((2, 4, tile, model_width), kind),
            pltpu.VMEM((rows, width), kind),
            pltpu.VMEM((2, rows, 2 * width), kind),
            pltpu.VMEM((4, 2, 2, rows, 2 * width), kind),
            stats,
            stats,
            stats,
            pltpu.VMEM((rows, width), kind),
            pltpu.VMEM((3, tile, model_width), kind),
            pltpu.VMEM((2, tile // 2, model_width), kind),
            pltpu.VMEM((2, tile, model_width), kind),
            pltpu.VMEM((tile, model_width), kind),
            pltpu.SemaphoreType.DMA((43,)),
            pltpu.SemaphoreType.DMA((43,)),
        ],
        compiler_params=pltpu.CompilerParams(collective_id=0, has_side_effects=True),
    )(length, state, modulation, gate, weights, out_weights)


def per_device(tokens, lengths, modulation, gate_gain, w_qkv, w_out):
    segment_count = lax.axis_size("segment")
    position = lax.axis_index("segment")
    parts_qkv = jnp.transpose(w_qkv[0], (1, 0, 2))
    state = tokens[0]
    for tick_index in range(TICKS):
        micro_index = (position - tick_index) % segment_count
        length = lax.dynamic_slice_in_dim(lengths, micro_index, 1, 0)
        state = layer(length, state, modulation[0], gate_gain, parts_qkv, w_out[0])
    return state[None]


def solution(mesh):
    return jax.shard_map(
        per_device,
        mesh=mesh,
        in_specs=(
            P("segment", ("seq", "head"), None),
            P(),
            P("segment", None, None),
            P("segment", None),
            P("segment", None, None, "head"),
            P("segment", "head", None),
        ),
        out_specs=P("segment", ("seq", "head"), None),
        check_vma=False,
    )
```

```python
import math

import jax
import jax.numpy as jnp
from jax import lax
from jax.experimental import pallas as pl
from jax.experimental.pallas import tpu as pltpu
from jax.sharding import PartitionSpec as P

HEAD = 128
TICKS = 2
PLANE = 8
MESH = pl.DeviceIdType.MESH
EXP2_SCALE = HEAD ** (-0.5) * math.log2(math.e)


def layer_norm(values):
    row_mean = jnp.mean(values, axis=-1, keepdims=True)
    centered = values - row_mean
    row_var = jnp.mean(centered * centered, axis=-1, keepdims=True)
    return centered / jnp.sqrt(row_var + 1e-06)


def remote(src, dst, send_sem, recv_sem, index, peer):
    return pltpu.make_async_remote_copy(
        src_ref=src,
        dst_ref=dst,
        send_sem=send_sem.at[index],
        recv_sem=recv_sem.at[index],
        device_id=peer,
        device_id_type=MESH,
    )


def ring_copies(source, target, here, behind, left, right, rows, send_sem, recv_sem, index):
    first, second = pl.ds(0, rows // 2), pl.ds(rows // 2, rows // 2)
    return {
        "right_first": remote(source.at[first], here(1).at[first], send_sem, recv_sem, index, right),
        "left_second": remote(source.at[second], here(3).at[second], send_sem, recv_sem, index + 1, left),
        "right_second": remote(source.at[second], here(1).at[second], send_sem, recv_sem, index + 2, right),
        "left_first": remote(source.at[first], here(3).at[first], send_sem, recv_sem, index + 3, left),
        "on_right": remote(behind(1).at[first], target(1).at[first], send_sem, recv_sem, index + 4, right),
        "on_left": remote(behind(3).at[second], target(3).at[second], send_sem, recv_sem, index + 5, left),
    }


FIRST_HOPS = ("right_first", "left_second", "right_second", "left_first")


def relay_kernel(
    length_ref, tokens_ref, modulation_ref, gate_ref, w_ref, out_w_ref, o_ref,
    states_ref, rows_all, q_ref, kv_ref, buf_all, max_ref, sum_ref, acc_ref, attended_ref, part_ref,
    relay_all, landed_all, updated_ref, send_all, recv_all,
):
    seq = lax.axis_index("seq")
    me = lax.axis_index("head")
    base = lax.div(seq, PLANE) * PLANE
    y = lax.rem(lax.div(seq, 2), 4)
    core = lax.rem(seq, 2)
    entry = pltpu.get_barrier_semaphore()
    peers = [
        {"head": lax.rem(me + 3, 4)},
        {"head": lax.rem(me + 1, 4)},
        {"seq": base + lax.rem(y + 3, 4) * 2 + core},
        {"seq": base + lax.rem(y + 1, 4) * 2 + core},
        {"seq": base + y * 2 + (1 - core)},
        {"seq": lax.rem(seq + PLANE, 2 * PLANE)},
        {"segment": lax.rem(lax.axis_index("segment") + 7, 8)},
    ]
    for peer in peers:
        pl.semaphore_signal(entry, inc=1, device_id=peer, device_id_type=MESH)
    states_ref[0] = tokens_ref[...]
    pl.semaphore_wait(entry, len(peers))

    def tick(t, carry):
        layer_body(
            length_ref[lax.rem(lax.axis_index("segment") + 8 - t, 8)], states_ref.at[t], states_ref.at[t + 1], modulation_ref, gate_ref, w_ref, out_w_ref,
            rows_all.at[t], q_ref, kv_ref, buf_all.at[t], max_ref, sum_ref, acc_ref, attended_ref, part_ref,
            relay_all.at[t], landed_all.at[t], updated_ref, send_all.at[t], recv_all.at[t],
        )
        return carry

    lax.fori_loop(0, TICKS, tick, 0)
    o_ref[...] = states_ref[TICKS]


def layer_body(
    length, state_ref, next_ref, modulation_ref, gate_ref, w_ref, out_w_ref,
    rows_ref, q_ref, kv_ref, buf, max_ref, sum_ref, acc_ref, attended_ref, part_ref, relay_ref,
    landed_ref, updated_ref, send_sem, recv_sem,
):
    seq = lax.axis_index("seq")
    me = lax.axis_index("head")
    half = lax.div(seq, PLANE)
    y = lax.rem(lax.div(seq, 2), 4)
    core = lax.rem(seq, 2)
    base = half * PLANE
    y_right = {"seq": base + lax.rem(y + 1, 4) * 2 + core}
    y_left = {"seq": base + lax.rem(y + 3, 4) * 2 + core}
    partner = {"seq": base + y * 2 + (1 - core)}
    far = {"seq": lax.rem(seq + PLANE, 2 * PLANE)}
    x_right_at, x_left_at = lax.rem(me + 1, 4), lax.rem(me + 3, 4)
    x_right, x_left = {"head": x_right_at}, {"head": x_left_at}
    x_opposite_at = lax.rem(me + 2, 4)
    position_at = lax.axis_index("segment")
    following = {"segment": lax.rem(position_at + 1, 8)}
    tile = state_ref.shape[0]
    rows = kv_ref.shape[1]
    width = q_ref.shape[1]
    heads = width // HEAD

    values = state_ref[...].astype(jnp.float32)
    shift = modulation_ref[0:1, :].astype(jnp.float32)
    scale = modulation_ref[1:2, :].astype(jnp.float32)
    rows_ref[0, me] = (layer_norm(values) * (1.0 + scale) + shift).astype(rows_ref.dtype)
    max_ref[...] = jnp.full_like(max_ref, -1e30)
    sum_ref[...] = jnp.zeros_like(sum_ref)
    acc_ref[...] = jnp.zeros_like(acc_ref)

    def x_copies(slot, source, index):
        def own(d):
            return rows_ref.at[slot, me]

        def neighbour(d):
            return rows_ref.at[slot, x_left_at] if d == 1 else rows_ref.at[slot, x_right_at]

        return ring_copies(source, neighbour, own, neighbour, x_left, x_right, tile, send_sem, recv_sem, index)

    def y_copies(slot, index):
        def landing(d):
            return buf.at[d, 0, slot]

        def opposite(d):
            return buf.at[2, 0, slot]

        copies = ring_copies(
            kv_ref.at[slot], opposite, landing, landing, y_left, y_right, rows, send_sem, recv_sem, index
        )
        first, second = pl.ds(0, rows // 2), pl.ds(rows // 2, rows // 2)
        across = {
            "across_own": (kv_ref.at[slot], buf.at[0, 1, slot]),
            "across_left": (buf.at[1, 0, slot], buf.at[1, 1, slot]),
            "across_right": (buf.at[3, 0, slot], buf.at[3, 1, slot]),
            "across_first": (buf.at[2, 0, slot, first], buf.at[2, 1, slot, first]),
            "across_second": (buf.at[2, 0, slot, second], buf.at[2, 1, slot, second]),
        }
        for offset, (name, (source, target)) in enumerate(across.items()):
            copies[name] = remote(source, target, send_sem, recv_sem, index + 6 + offset, partner)
        return copies

    top, bottom = pl.ds(0, tile // 2), pl.ds(tile // 2, tile // 2)
    swap_top = remote(rows_ref.at[0, me, top], rows_ref.at[1, me, top], send_sem, recv_sem, 0, far)
    swap_bottom = remote(rows_ref.at[0, me, bottom], rows_ref.at[1, me, bottom], send_sem, recv_sem, 35, far)
    x_own = x_copies(0, rows_ref.at[0, me], 1)
    x_far = x_copies(1, rows_ref.at[1, me], 7)
    y_own = y_copies(0, 13)
    y_far = y_copies(1, 24)

    def send_first(copies):
        for name in FIRST_HOPS:
            copies[name].start()

    def pass_on(copies):
        copies["right_first"].wait_recv()
        copies["on_right"].start()
        copies["left_second"].wait_recv()
        copies["on_left"].start()

    def rest_of_x(copies):
        for name in ("right_second", "left_first", "on_right", "on_left"):
            copies[name].wait_recv()

    def neighbours_across(copies):
        copies["right_second"].wait_recv()
        copies["across_left"].start()
        copies["left_first"].wait_recv()
        copies["across_right"].start()

    def opposite_across(copies):
        copies["on_right"].wait_recv()
        copies["across_first"].start()
        copies["on_left"].wait_recv()
        copies["across_second"].start()

    def project(slot, group):
        block = rows_ref[slot].reshape(rows, rows_ref.shape[3])
        return jnp.dot(block, w_ref[group], preferred_element_type=jnp.float32).astype(jnp.bfloat16)

    def project_kv(slot):
        def one(part, carry):
            kv_ref[slot, :, pl.ds(pl.multiple_of(part * width, HEAD), width)] = project(slot, part + 1)
            return carry

        lax.fori_loop(0, 2, one, 0)

    def attend_shard(shard, behind, other_core, slot):
        source = lax.rem(y + 4 - behind, 4) * 2 + lax.rem(core + other_core, 2)
        which = half if slot == 0 else 1 - half
        position = lax.broadcasted_iota(jnp.int32, (1, rows), 1) + (which * PLANE + source) * rows
        valid = position < length

        def one_head(h, carry):
            k_columns = pl.ds(pl.multiple_of(h * HEAD, HEAD), HEAD)
            v_columns = pl.ds(pl.multiple_of((heads + h) * HEAD, HEAD), HEAD)
            scores = lax.dot_general(
                q_ref[:, k_columns],
                shard[:, k_columns],
                (((1,), (1,)), ((), ())),
                preferred_element_type=jnp.float32,
            )
            scores = jnp.where(valid, scores * EXP2_SCALE, -1e30)
            old_max = max_ref[h]
            new_max = jnp.maximum(old_max, jnp.max(scores, axis=1, keepdims=True))
            rescale = jnp.exp2(old_max - new_max)
            weights = jnp.exp2(scores - new_max[:, :1])
            max_ref[h] = new_max
            sum_ref[h] = sum_ref[h] * rescale + jnp.sum(weights, axis=1, keepdims=True)
            acc_ref[h] = acc_ref[h] * rescale + jnp.dot(
                weights.astype(jnp.bfloat16), shard[:, v_columns], preferred_element_type=jnp.float32
            )
            return carry

        lax.fori_loop(0, heads, one_head, 0)

    def attend_buf(behind, other_core, slot):
        attend_shard(buf.at[behind, other_core, slot], behind, other_core, slot)

    swap_top.start()
    swap_bottom.start()
    send_first(x_own)
    pass_on(x_own)
    rest_of_x(x_own)
    project_kv(0)
    send_first(y_own)
    y_own["across_own"].start()
    q_ref[...] = project(0, 0)
    attend_shard(kv_ref.at[0], 0, 0, 0)
    pass_on(y_own)
    swap_top.wait_recv()
    x_far["right_first"].start()
    x_far["left_first"].start()
    neighbours_across(y_own)
    swap_bottom.wait_recv()
    x_far["left_second"].start()
    x_far["right_second"].start()
    y_own["across_own"].wait_recv()
    attend_buf(0, 1, 0)
    pass_on(x_far)
    attend_buf(1, 0, 0)
    attend_buf(3, 0, 0)
    opposite_across(y_own)
    rest_of_x(x_far)
    project_kv(1)
    send_first(y_far)
    y_far["across_own"].start()
    attend_shard(kv_ref.at[1], 0, 0, 1)
    y_own["across_left"].wait_recv()
    attend_buf(1, 1, 0)
    pass_on(y_far)
    y_own["across_right"].wait_recv()
    attend_buf(3, 1, 0)
    attend_buf(2, 0, 0)
    neighbours_across(y_far)
    y_own["across_first"].wait_recv()
    y_own["across_second"].wait_recv()
    attend_buf(2, 1, 0)
    y_far["across_own"].wait_recv()
    attend_buf(0, 1, 1)
    attend_buf(1, 0, 1)
    opposite_across(y_far)
    attend_buf(3, 0, 1)
    y_far["across_left"].wait_recv()
    attend_buf(1, 1, 1)
    y_far["across_right"].wait_recv()
    attend_buf(3, 1, 1)
    attend_buf(2, 0, 1)
    y_far["across_first"].wait_recv()
    y_far["across_second"].wait_recv()
    attend_buf(2, 1, 1)
    for h in range(heads):
        attended_ref[:, h * HEAD : (h + 1) * HEAD] = (acc_ref[h] / sum_ref[h]).astype(attended_ref.dtype)

    def branch_of(device):
        block = attended_ref[pl.ds(pl.multiple_of(device * tile, tile), tile), :]
        return jnp.dot(block, out_w_ref[...], preferred_element_type=jnp.float32)

    to_right = remote(part_ref.at[0, top], relay_ref.at[0], send_sem, recv_sem, 36, x_right)
    to_left = remote(part_ref.at[0, bottom], relay_ref.at[1], send_sem, recv_sem, 37, x_left)
    plain_right = remote(part_ref.at[1, bottom], landed_ref.at[0, bottom], send_sem, recv_sem, 38, x_right)
    plain_left = remote(part_ref.at[2, top], landed_ref.at[1, top], send_sem, recv_sem, 39, x_left)
    sum_right = remote(part_ref.at[1, top], landed_ref.at[0, top], send_sem, recv_sem, 40, x_right)
    sum_left = remote(part_ref.at[2, bottom], landed_ref.at[1, bottom], send_sem, recv_sem, 41, x_left)
    onward = remote(updated_ref, next_ref, send_sem, recv_sem, 42, following)
    part_ref[0] = branch_of(x_opposite_at).astype(part_ref.dtype)
    to_right.start()
    to_left.start()
    part_ref[1] = branch_of(x_right_at).astype(part_ref.dtype)
    plain_right.start()
    part_ref[2] = branch_of(x_left_at).astype(part_ref.dtype)
    plain_left.start()
    to_right.wait_recv()
    part_ref[1, top, :] = (
        part_ref[1, top, :].astype(jnp.float32) + relay_ref[0].astype(jnp.float32)
    ).astype(part_ref.dtype)
    sum_right.start()
    to_left.wait_recv()
    part_ref[2, bottom, :] = (
        part_ref[2, bottom, :].astype(jnp.float32) + relay_ref[1].astype(jnp.float32)
    ).astype(part_ref.dtype)
    sum_left.start()
    branch = branch_of(me)
    for copy in (plain_right, plain_left, sum_right, sum_left):
        copy.wait_recv()
    branch = branch + landed_ref[0].astype(jnp.float32) + landed_ref[1].astype(jnp.float32)
    updated_ref[...] = (
        state_ref[...].astype(jnp.float32) + gate_ref[...].astype(jnp.float32) * branch
    ).astype(updated_ref.dtype)
    onward.start()
    for copy in (swap_top, swap_bottom, to_right, to_left, plain_right, plain_left, sum_right, sum_left):
        copy.wait_send()
    for copies in (x_own, x_far, y_own, y_far):
        for copy in copies.values():
            copy.wait_send()
    onward.wait()


def relay(length, state, modulation, gate, weights, out_weights):
    tile, model_width = state.shape
    width = weights.shape[2]
    rows = 4 * tile
    kind = state.dtype
    vmem = pl.BlockSpec(memory_space=pltpu.VMEM)
    stats = pltpu.VMEM((width // HEAD, rows, HEAD), jnp.float32)
    return pl.pallas_call(
        relay_kernel,
        in_specs=[pl.BlockSpec(memory_space=pltpu.SMEM), vmem, vmem, vmem, vmem, vmem],
        out_specs=vmem,
        out_shape=jax.ShapeDtypeStruct(state.shape, kind),
        scratch_shapes=[
            pltpu.VMEM((TICKS + 1, tile, model_width), kind),
            pltpu.VMEM((TICKS, 2, 4, tile, model_width), kind),
            pltpu.VMEM((rows, width), kind),
            pltpu.VMEM((2, rows, 2 * width), kind),
            pltpu.VMEM((TICKS, 4, 2, 2, rows, 2 * width), kind),
            stats,
            stats,
            stats,
            pltpu.VMEM((rows, width), kind),
            pltpu.VMEM((3, tile, model_width), kind),
            pltpu.VMEM((TICKS, 2, tile // 2, model_width), kind),
            pltpu.VMEM((TICKS, 2, tile, model_width), kind),
            pltpu.VMEM((tile, model_width), kind),
            pltpu.SemaphoreType.DMA((TICKS, 43)),
            pltpu.SemaphoreType.DMA((TICKS, 43)),
        ],
        compiler_params=pltpu.CompilerParams(collective_id=0, has_side_effects=True),
    )(length, state, modulation, gate, weights, out_weights)


def per_device(tokens, lengths, modulation, gate_gain, w_qkv, w_out):
    parts_qkv = jnp.transpose(w_qkv[0], (1, 0, 2))
    state = relay(lengths, tokens[0], modulation[0], gate_gain, parts_qkv, w_out[0])
    return state[None]


def solution(mesh):
    return jax.shard_map(
        per_device,
        mesh=mesh,
        in_specs=(
            P("segment", ("seq", "head"), None),
            P(),
            P("segment", None, None),
            P("segment", None),
            P("segment", None, None, "head"),
            P("segment", "head", None),
        ),
        out_specs=P("segment", ("seq", "head"), None),
        check_vma=False,
    )
```
